256 devices in a mesh: users: 64 (over x, z, y_hi), items: 4 (over y_lo, core).
Axes of the slice: x: 4, y: 4 (y_hi: 2, y_lo: 2; y = y_hi * 2 + y_lo), z: 8, core: 2. Of those that a mesh axis runs over, the one named last changes fastest.
Arguments:
- user_factors: bfloat16 [131072, 128], P('users'), may hold values from -0.5 to 0.5
- item_factors: float32 [4, 4, 512, 128], P('items', None, 'users'), may hold values from -6 to 6
- tile_user: int32 [64, 4, 4, 16], P('users', 'items'), may hold values from 0 to 7, as said below
- tile_item: int32 [64, 4, 4, 16], P('users', 'items'), may hold values from 0 to 1, as said below
- tile_count: int32 [64, 4, 4], P('users', 'items'), may hold values from 1 to 16, as said below
- ratings: bfloat16 [64, 4, 4, 16, 256, 256], P('users', 'items'), may hold values from -6 to 6
- mask: int32 [64, 4, 4, 16, 32, 256], P('users', 'items'), may hold values from 0 to 255
Outputs:
- new_items: float32 [4, 4, 512, 128], P('items', None, 'users')
- user_grad: float32 [131072, 128], P(('users', 'items'))
The draws below stay inside these ranges and needn't reach their ends.
Inputs may be any that keep to these rules, and one draw needn't show every extreme that they name: `tile_user`: index of a user tile within its user block. `tile_item`: index of an item tile within its panel; the pairs (tile_user, tile_item) of one user block, owner and panel are distinct. Only the first tile_count slots of a user block, owner and panel hold observed tiles; the other slots are to be ignored. For every owner and panel some user block fills all 16 slots. Bit k of word mask[..., w, j] marks the rating in row 8 * w + k, column j of the tile as observed.
All inputs are finite; a program needn't handle non-finite values.
Results may differ from the reference program's by a relative error of at most 0.0031.
Values may be sent and summed in bfloat16 or wider, within the bound.
A program may use at most 128 MiB of HBM per device.

```python
import math
import jax
import jax.numpy as jnp
from jax import lax

R = 128
TILE = 256
UT_DEV = 8
IT_PAN = 2
STEPS = 4
SLOTS = 16
UBLOCKS = 64
IOWN = 4
USER_DEV = 2048
USERS = 131072
PANEL_ROWS = 512
WORDS = 32


def draw_pairs(key):
    cell_count = UT_DEV * IT_PAN
    scores = jax.random.randint(jax.random.fold_in(key, 11), (UBLOCKS, IOWN, STEPS, cell_count), 0, 4096)
    distinct = scores * cell_count + jnp.arange(cell_count, dtype=jnp.int32)
    ordered = jnp.argsort(distinct, axis=-1, stable=True)[..., :SLOTS]
    return ordered.astype(jnp.int32)


def draw_tile_user(key, part):
    return (draw_pairs(key) // IT_PAN).astype(jnp.int32)


def draw_tile_item(key, part):
    return (draw_pairs(key) % IT_PAN).astype(jnp.int32)


def draw_tile_count(key, part):
    base_count = jax.random.randint(jax.random.fold_in(key, 21), (UBLOCKS, IOWN, STEPS), 1, SLOTS // 2 + 1)
    heavy_draw = jax.random.randint(jax.random.fold_in(key, 22), (UBLOCKS, IOWN, STEPS), 0, 8)
    chosen = jax.random.randint(jax.random.fold_in(key, 23), (IOWN, STEPS), 0, UBLOCKS)
    block_iota = jnp.arange(UBLOCKS, dtype=jnp.int32)[:, None, None]
    full_slots = (heavy_draw == 0) | (block_iota == chosen[None])
    return jnp.where(full_slots, SLOTS, base_count).astype(jnp.int32)


def place_ends(array, rng, low, top_value):
    longest = array.shape.index(max(array.shape))
    spots = []
    for shift in (0, 1):
        where = [jax.random.randint(jax.random.fold_in(rng, axis), (), 0, length) for axis, length in enumerate(array.shape)]
        where[longest] = (where[longest] + shift) % array.shape[longest]
        spots.append(tuple(where))
    return array.at[spots[0]].set(low).at[spots[1]].set(top_value)


def steps_of(key, dims, shards, smallest, largest):
    def one(dim, shards_of):
        steps = jax.random.uniform(jax.random.fold_in(jax.random.fold_in(key, 6), dim), (shards_of,), jnp.float32, smallest / len(shards), largest / len(shards))
        return jnp.repeat(jnp.exp(steps), dims[dim] // shards_of).reshape((-1,) + (1,) * (len(dims) - dim - 1))

    loudness = one(*shards[0])
    for cut in shards[1:]:
        loudness = loudness * one(*cut)
    return loudness


def scatter_about(stream_key, extent, spread, reach, shards=(), kind=jnp.bfloat16):
    entries = spread * jax.random.normal(stream_key, extent, jnp.float32)
    if shards:
        entries = entries * steps_of(stream_key, extent, shards, -0.22, 0.18)
    return jnp.clip(entries, -reach, reach).astype(kind)


def setup_inputs(seed: int = 0) -> dict:
    key_list = jax.random.split(jax.random.key(seed), 8)
    return {
        "user_factors": scatter_about(key_list[0], (USERS, R), R ** -0.5, 0.5, ((0, 64),)),
        "item_factors": scatter_about(key_list[1], (IOWN, STEPS, PANEL_ROWS, R), 1.0, 6.0, ((0, 4), (2, 64)), jnp.float32),
        "tile_user": draw_tile_user(jax.random.fold_in(key_list[7], 71), 0),
        "tile_item": draw_tile_item(jax.random.fold_in(key_list[7], 71), 0),
        "tile_count": draw_tile_count(jax.random.fold_in(key_list[7], 71), 0),
        "ratings": scatter_about(key_list[5], (UBLOCKS, IOWN, STEPS, SLOTS, TILE, TILE), 1.0, 6.0, ((0, 64), (1, 4))),
        "mask": place_ends(jax.random.randint(key_list[6], (UBLOCKS, IOWN, STEPS, SLOTS, WORDS, TILE), 0, 256), jax.random.fold_in(key_list[6], 1), 0, 255).astype(jnp.int32),
    }


def reference(user_factors, item_factors, tile_user, tile_item, tile_count, ratings, mask):
    shifts = jnp.arange(8, dtype=jnp.int32)
    user_blocks = user_factors.reshape(UBLOCKS, UT_DEV, TILE, R)
    panel_bf = item_factors.astype(jnp.bfloat16)
    step_rate = 8.0 / math.sqrt(TILE * UBLOCKS)

    def one_block(panel_grad, inputs):
        block_rows, block_user, block_item, block_count, block_ratings, block_mask = inputs
        user_sum = jnp.zeros((UT_DEV, TILE, R), jnp.float32)
        for owner_index in range(IOWN):
            for step_index in range(STEPS):
                user_index = block_user[owner_index, step_index].astype(jnp.int32)
                item_index = block_item[owner_index, step_index].astype(jnp.int32)
                user_rows = block_rows[user_index].astype(jnp.float32)
                panel_tiles = panel_bf[owner_index, step_index].reshape(IT_PAN, TILE, R)
                item_rows = panel_tiles[item_index].astype(jnp.float32)
                predicted = jnp.einsum('tir,tjr->tij', user_rows, item_rows, precision=lax.Precision.HIGHEST)
                mask_bits = block_mask[owner_index, step_index][:, :, None, :] >> shifts[None, None, :, None] & 1
                observed = mask_bits.reshape(SLOTS, TILE, TILE).astype(jnp.float32)
                live_slots = (jnp.arange(SLOTS) < block_count[owner_index, step_index]).astype(jnp.float32)
                errors = (observed * live_slots[:, None, None] * (predicted - block_ratings[owner_index, step_index].astype(jnp.float32))).astype(jnp.bfloat16)
                errors = lax.optimization_barrier(errors).astype(jnp.float32)
                tile_grad = jnp.einsum('tij,tir->tjr', errors, user_rows, precision=lax.Precision.HIGHEST)
                panel_grad = panel_grad.at[owner_index, step_index, item_index].add(tile_grad)
                user_part = jnp.einsum('tij,tjr->tir', errors, item_rows, precision=lax.Precision.HIGHEST)
                user_sum = user_sum.at[user_index].add(user_part)
        return (panel_grad, user_sum.reshape(USER_DEV, R) / 32.0)
    start = jnp.zeros((IOWN, STEPS, IT_PAN, TILE, R), jnp.float32)
    panel_grad, user_parts = lax.scan(one_block, start, (user_blocks, tile_user, tile_item, tile_count, ratings, mask))
    new_items = 0.95 * item_factors - step_rate * panel_grad.reshape(IOWN, STEPS, PANEL_ROWS, R)
    return (new_items, user_parts.reshape(USERS, R))
```

```python
import functools
import math

import jax
import jax.numpy as jnp
from jax import lax
from jax.experimental import pallas as pl
from jax.experimental.pallas import tpu as pltpu
from jax.sharding import PartitionSpec as P

MESH = pl.DeviceIdType.MESH
XS, ZS, YS = 4, 8, 2
ITEMS = 4
STEPS = 4
SLOTS = 16
TILE = 256
UTILES = 8
RANK = 128
ROWS = 8
QROWS = 128
ZY = ZS * YS
F32, BF16 = jnp.float32, jnp.bfloat16


def kernel(
    tile_user, tile_item, tile_count, items, factors, ratings, mask,
    new_items, user_grad,
    slots, lives, cells, rat_v, mask_v, uf, uft, panel, other, err, gacc,
    own_grad, grad_out, grad_in, sums, zy_out, zy_in, user_sum, user_out, user_in,
    load_sem, y_sem, zs_sem, zr_sem, xs_sem, xr_sem, gs_sem, gr_sem,
    zys_sem, zyr_sem, us_sem, ur_sem,
):
    me = lax.axis_index("users")
    it = lax.axis_index("items")
    xi = lax.div(me, ZY)
    zy = lax.rem(me, ZY)
    zi = lax.div(zy, YS)
    yi = lax.rem(zy, YS)

    def at_users(x, z, y):
        return {"users": x * ZY + z * YS + y}

    def ring(value, step, size):
        return lax.rem(value + step, size)

    loads = [pltpu.make_async_copy(factors, uf, load_sem.at[16])]
    for s in range(STEPS):
        for half in range(2):
            lanes = pl.ds(half * 128, 128)
            rows = pl.ds(s * SLOTS, SLOTS)
            loads.append(pltpu.make_async_copy(
                mask.at[0, 0, s, :, :, lanes], mask_v.at[half, rows], load_sem.at[s * 2 + half]))
            loads.append(pltpu.make_async_copy(
                ratings.at[0, 0, s, :, :, lanes], rat_v.at[half, rows], load_sem.at[8 + s * 2 + half]))

    barrier = pltpu.get_barrier_semaphore()
    greeted = 0
    for d in range(1, ZY):
        pl.semaphore_signal(barrier, inc=1, device_id={"users": xi * ZY + ring(zy, d, ZY)}, device_id_type=MESH)
        greeted += 1
    for d in range(1, XS):
        pl.semaphore_signal(barrier, inc=1, device_id={"users": ring(xi, d, XS) * ZY + zy}, device_id_type=MESH)
        greeted += 1
    for d in range(1, ITEMS):
        pl.semaphore_signal(barrier, inc=1, device_id={"items": ring(it, d, ITEMS)}, device_id_type=MESH)
        greeted += 1
    for load in loads:
        load.start()
    pl.semaphore_wait(barrier, greeted)

    y_copy = pltpu.make_async_remote_copy(
        src_ref=items.at[0], dst_ref=other, send_sem=y_sem.at[0], recv_sem=y_sem.at[1],
        device_id=at_users(xi, zi, 1 - yi), device_id_type=MESH)
    y_copy.start()

    for s in range(STEPS):
        for t in range(SLOTS):
            cell = tile_user[0, 0, s, t] * 2 + tile_item[0, 0, s, t]
            cells[s * SLOTS + t] = jnp.where(t < tile_count[0, 0, s], cell, -1)

    @pl.loop(0, STEPS * SLOTS)
    def _(idx):
        first = lax.div(idx, SLOTS) * SLOTS
        cell = lax.rem(idx, SLOTS)
        slot = jnp.int32(0)
        live = jnp.int32(0)
        for t in range(SLOTS):
            hit = cells[first + t] == cell
            slot = jnp.where(hit, t, slot)
            live = jnp.where(hit, -1, live)
        slots[idx] = slot
        lives[idx] = live

    user_sum[...] = jnp.zeros_like(user_sum)

    y_copy.wait_recv()
    mine = items[0]
    theirs = other[...]
    low = jnp.where(yi == 0, mine, theirs)
    high = jnp.where(yi == 0, theirs, mine)
    my_rows = pl.ds(pl.multiple_of(zi * 16, 16), 16)
    panel[xi, :, my_rows, :] = jnp.concatenate([low, high], axis=1).astype(BF16)

    z_copies = []
    for d in (4, 3, 5, 2, 6, 1, 7):
        part = panel.at[xi, :, my_rows, :]
        copy = pltpu.make_async_remote_copy(
            src_ref=part, dst_ref=part, send_sem=zs_sem.at[d], recv_sem=zr_sem.at[d],
            device_id=at_users(xi, ring(zi, d, ZS), yi), device_id_type=MESH)
        copy.start()
        z_copies.append(copy)

    for load in loads:
        load.wait()
    uft[...] = uf[...].T

    for copy in z_copies:
        copy.wait_recv()

    def x_copy(h, d):
        part = panel.at[xi, pl.ds(2 * h, 2)]
        return pltpu.make_async_remote_copy(
            src_ref=part, dst_ref=part, send_sem=xs_sem.at[h, d], recv_sem=xr_sem.at[h, d],
            device_id=at_users(ring(xi, d, XS), zi, yi), device_id_type=MESH)

    for h in range(2):
        for d in (1, 3, 2):
            x_copy(h, d).start()

    bits = jnp.left_shift(jnp.int32(1), lax.broadcasted_iota(jnp.int32, (1, 8, 128), 1))

    def g_copy(h, d):
        return pltpu.make_async_remote_copy(
            src_ref=grad_out.at[h, d], dst_ref=grad_in.at[h, d],
            send_sem=gs_sem.at[h, d], recv_sem=gr_sem.at[h, d],
            device_id=at_users(ring(xi, d, XS), zi, yi), device_id_type=MESH)

    def chunk(q, h):
        pair = panel[q, pl.ds(2 * h, 2)].reshape(2 * QROWS, RANK)
        half = lax.rem(q, 2)
        p = lax.div(q, 2)
        for u in range(UTILES):
            span = pl.ds(u * TILE, TILE)
            predicted = lax.dot_general(
                uf[span, :], pair, (((1,), (1,)), ((), ())), preferred_element_type=F32)
            parts = []
            for k in range(2):
                first = (2 * h + k) * SLOTS
                slot = first + slots[first + 2 * u + p]
                live = lives[first + 2 * u + p]
                words = mask_v[half, slot] & live
                seen = (jnp.broadcast_to(words[:, None, :], (32, 8, 128)) & bits) != 0
                gap = predicted[:, k * 128:(k + 1) * 128] - rat_v[half, slot].astype(F32)
                kept = jnp.where(seen, gap.reshape(32, 8, 128), 0.0)
                parts.append(kept.reshape(TILE, 128).astype(BF16))
            errors = jnp.concatenate(parts, axis=1)
            err[span, :] = errors
            user_sum[span, :] += jnp.dot(errors, pair, preferred_element_type=F32)
        gacc[...] = jnp.dot(uft[...], err[...], preferred_element_type=F32)
        return gacc[...].T.reshape(2, QROWS, RANK)

    @pl.loop(0, 8)
    def _(c):
        h = lax.div(c, 4)
        k = lax.rem(c, 4)
        d = jnp.where(h == 0, jnp.where(k == 3, 2, jnp.where(k == 2, 3, k)),
                      jnp.where(k == 3, 0, jnp.where(k == 2, 3, 2 - k)))
        q = ring(xi, d, XS)

        @pl.when(d != 0)
        def _():
            x_copy(h, XS - d).wait_recv()

        grad = chunk(q, h)

        @pl.when(d == 0)
        def _():
            own_grad[h] = grad

        @pl.when(d != 0)
        def _():
            grad_out[h, d] = grad.astype(BF16)
            g_copy(h, d).start()

    def u_copy(d):
        return pltpu.make_async_remote_copy(
            src_ref=user_out.at[d], dst_ref=user_in.at[d],
            send_sem=us_sem.at[d], recv_sem=ur_sem.at[d],
            device_id={"items": ring(it, d, ITEMS)}, device_id_type=MESH)

    share = 2 * TILE
    for d in (2, 3, 1):
        rows = pl.ds(pl.multiple_of(ring(it, d, ITEMS) * share, share), share)
        user_out[d] = user_sum[rows, :].astype(BF16)
        u_copy(d).start()

    def zy_copy(h, d):
        return pltpu.make_async_remote_copy(
            src_ref=zy_out.at[h, d], dst_ref=zy_in.at[h, d],
            send_sem=zys_sem.at[h, d], recv_sem=zyr_sem.at[h, d],
            device_id={"users": xi * ZY + ring(zy, d, ZY)}, device_id_type=MESH)

    for h in range(2):
        for d in range(1, XS):
            g_copy(h, d).wait_recv()
        sums[h] = own_grad[h] + (
            grad_in[h, 1].astype(F32) + grad_in[h, 2].astype(F32) + grad_in[h, 3].astype(F32))
        for d in range(1, ZY):
            rows = pl.ds(pl.multiple_of(ring(zy, d, ZY) * ROWS, ROWS), ROWS)
            zy_out[h, d] = sums[h, :, rows, :].reshape(2 * ROWS, RANK).astype(BF16)
        for d in (8, 7, 9, 6, 10, 5, 11, 4, 12, 3, 13, 2, 14, 1, 15):
            zy_copy(h, d).start()

    my_share = pl.ds(pl.multiple_of(it * share, share), share)
    for d in range(1, ITEMS):
        u_copy(d).wait_recv()
    user_grad[...] = (user_sum[my_share, :] + (
        user_in[1].astype(F32) + user_in[2].astype(F32) + user_in[3].astype(F32))) * (1.0 / 32.0)

    step_rate = 8.0 / math.sqrt(TILE * XS * ZY)
    mine_rows = pl.ds(pl.multiple_of(zy * ROWS, ROWS), ROWS)
    for h in range(2):
        total = sums[h, :, mine_rows, :].reshape(2 * ROWS, RANK)
        for d in range(1, ZY):
            zy_copy(h, d).wait_recv()
            total = total + zy_in[h, d].astype(F32)
        pair = pl.ds(2 * h, 2)
        new_items[0, pair] = 0.95 * items[0, pair] - step_rate * total.reshape(2, ROWS, RANK)

    y_copy.wait_send()
    for copy in z_copies:
        copy.wait_send()
    for h in range(2):
        for d in range(1, XS):
            x_copy(h, d).wait_send()
            g_copy(h, d).wait_send()
        for d in range(1, ZY):
            zy_copy(h, d).wait_send()
    for d in range(1, ITEMS):
        u_copy(d).wait_send()


def shards(user_factors, item_factors, tile_user, tile_item, tile_count, ratings, mask):
    smem = pl.BlockSpec(memory_space=pltpu.SMEM)
    vmem = pl.BlockSpec(memory_space=pltpu.VMEM)
    hbm = pl.BlockSpec(memory_space=pl.ANY)
    dma = pltpu.SemaphoreType.DMA
    return pl.pallas_call(
        kernel,
        out_shape=(
            jax.ShapeDtypeStruct(item_factors.shape, F32),
            jax.ShapeDtypeStruct((user_factors.shape[0] // ITEMS, RANK), F32),
        ),
        in_specs=[smem, smem, smem, vmem, hbm, hbm, hbm],
        out_specs=(vmem, vmem),
        scratch_shapes=[
            pltpu.SMEM((STEPS * SLOTS,), jnp.int32),
            pltpu.SMEM((STEPS * SLOTS,), jnp.int32),
            pltpu.SMEM((STEPS * SLOTS,), jnp.int32),
            pltpu.VMEM((2, STEPS * SLOTS, TILE, 128), BF16),
            pltpu.VMEM((2, STEPS * SLOTS, TILE // 8, 128), jnp.int32),
            pltpu.VMEM((UTILES * TILE, RANK), BF16),
            pltpu.VMEM((RANK, UTILES * TILE), BF16),
            pltpu.VMEM((XS, STEPS, QROWS, RANK), BF16),
            pltpu.VMEM((STEPS, ROWS, RANK), F32),
            pltpu.VMEM((UTILES * TILE, 2 * QROWS), BF16),
            pltpu.VMEM((RANK, 2 * QROWS), F32),
            pltpu.VMEM((2, 2, QROWS, RANK), F32),
            pltpu.VMEM((2, XS, 2, QROWS, RANK), BF16),
            pltpu.VMEM((2, XS, 2, QROWS, RANK), BF16),
            pltpu.VMEM((2, 2, QROWS, RANK), F32),
            pltpu.VMEM((2, ZY, 2 * ROWS, RANK), BF16),
            pltpu.VMEM((2, ZY, 2 * ROWS, RANK), BF16),
            pltpu.VMEM((UTILES * TILE, RANK), F32),
            pltpu.VMEM((ITEMS, 2 * TILE, RANK), BF16),
            pltpu.VMEM((ITEMS, 2 * TILE, RANK), BF16),
            dma((17,)), dma((2,)), dma((ZS,)), dma((ZS,)),
            dma((2, XS)), dma((2, XS)), dma((2, XS)), dma((2, XS)),
            dma((2, ZY)), dma((2, ZY)), dma((ITEMS,)), dma((ITEMS,)),
        ],
        compiler_params=pltpu.CompilerParams(
            collective_id=0, has_side_effects=True, vmem_limit_bytes=40 * 2**20),
        name="factor_step",
    )(tile_user, tile_item, tile_count, item_factors, user_factors, ratings, mask)


def solution(mesh):
    return jax.shard_map(
        shards,
        mesh=mesh,
        in_specs=(
            P("users", None),
            P("items", None, "users", None),
            P("users", "items", None, None),
            P("users", "items", None, None),
            P("users", "items", None),
            P("users", "items", None, None, None, None),
            P("users", "items", None, None, None, None),
        ),
        out_specs=(P("items", None, "users", None), P(("users", "items"), None)),
        check_vma=False,
    )
```

```python
import functools
import math

import jax
import jax.numpy as jnp
from jax import lax
from jax.experimental import pallas as pl
from jax.experimental.pallas import tpu as pltpu
from jax.sharding import PartitionSpec as P

MESH = pl.DeviceIdType.MESH
XS, ZS, YS = 4, 8, 2
ITEMS = 4
STEPS = 4
SLOTS = 16
TILE = 256
UTILES = 8
RANK = 128
ROWS = 8
QROWS = 128
ZY = ZS * YS
F32, BF16 = jnp.float32, jnp.bfloat16


def kernel(
    tile_user_hbm, tile_item_hbm, tile_count_hbm, items_hbm, factors, ratings, mask,
    new_items, user_grad,
    tile_user, tile_item, tile_count, items,
    slots, lives, cells, rat_v, mask_v, uf, uft, panel, other, err, gacc,
    own_grad, grad_out, grad_in, sums, zy_out, zy_in, user_sum, user_out, user_in,
    load_sem, y_sem, zs_sem, zr_sem, xs_sem, xr_sem, gs_sem, gr_sem,
    zys_sem, zyr_sem, us_sem, ur_sem,
):
    me = lax.axis_index("users")
    it = lax.axis_index("items")
    xi = lax.div(me, ZY)
    zy = lax.rem(me, ZY)
    zi = lax.div(zy, YS)
    yi = lax.rem(zy, YS)

    def at_users(x, z, y):
        return {"users": x * ZY + z * YS + y}

    def ring(value, step, size):
        return lax.rem(value + step, size)

    tables = [
        pltpu.make_async_copy(tile_user_hbm, tile_user, load_sem.at[9]),
        pltpu.make_async_copy(tile_item_hbm, tile_item, load_sem.at[10]),
        pltpu.make_async_copy(tile_count_hbm, tile_count, load_sem.at[11]),
        pltpu.make_async_copy(items_hbm, items, load_sem.at[12]),
    ]
    loads = [pltpu.make_async_copy(factors, uf, load_sem.at[8])]
    for s in range(STEPS):
        rows = pl.ds(s * SLOTS, SLOTS)
        loads.append(pltpu.make_async_copy(mask.at[0, 0, s], mask_v.at[rows], load_sem.at[s]))
        loads.append(pltpu.make_async_copy(ratings.at[0, 0, s], rat_v.at[rows], load_sem.at[4 + s]))

    barrier = pltpu.get_barrier_semaphore()
    greeted = 0
    pl.semaphore_signal(barrier, inc=1, device_id=at_users(xi, zi, 1 - yi), device_id_type=MESH)
    greeted += 1
    for d in range(1, ZS):
        pl.semaphore_signal(barrier, inc=1, device_id=at_users(xi, ring(zi, d, ZS), yi), device_id_type=MESH)
        greeted += 1
    for d in range(1, XS):
        pl.semaphore_signal(barrier, inc=1, device_id={"users": ring(xi, d, XS) * ZY + zy}, device_id_type=MESH)
        greeted += 1
    for d in range(1, ITEMS):
        pl.semaphore_signal(barrier, inc=1, device_id={"items": ring(it, d, ITEMS)}, device_id_type=MESH)
        greeted += 1
    for load in tables + loads:
        load.start()
    for load in tables:
        load.wait()

    for s in range(STEPS):
        for t in range(SLOTS):
            cell = tile_user[0, 0, s, t] * 2 + tile_item[0, 0, s, t]
            cells[s * SLOTS + t] = jnp.where(t < tile_count[0, 0, s], cell, -1)

    @pl.loop(0, STEPS * SLOTS)
    def _(idx):
        first = lax.div(idx, SLOTS) * SLOTS
        cell = lax.rem(idx, SLOTS)
        slot = jnp.int32(0)
        live = jnp.int32(0)
        for t in range(SLOTS):
            hit = cells[first + t] == cell
            slot = jnp.where(hit, t, slot)
            live = jnp.where(hit, -1, live)
        slots[idx] = slot
        lives[idx] = live

    user_sum[...] = jnp.zeros_like(user_sum)

    pl.semaphore_wait(barrier, greeted)

    y_copy = pltpu.make_async_remote_copy(
        src_ref=items_hbm.at[0], dst_ref=other, send_sem=y_sem.at[0], recv_sem=y_sem.at[1],
        device_id=at_users(xi, zi, 1 - yi), device_id_type=MESH)
    y_copy.start()

    y_copy.wait_recv()
    mine = items[0]
    theirs = other[...]
    low = jnp.where(yi == 0, mine, theirs)
    high = jnp.where(yi == 0, theirs, mine)
    my_rows = pl.ds(pl.multiple_of(zi * 16, 16), 16)
    panel[xi, :, my_rows, :] = jnp.concatenate([low, high], axis=1).astype(BF16)

    def z_copy(h, d):
        part = panel.at[xi, pl.ds(2 * h, 2), my_rows, :]
        return pltpu.make_async_remote_copy(
            src_ref=part, dst_ref=part, send_sem=zs_sem.at[h, d], recv_sem=zr_sem.at[h, d],
            device_id=at_users(xi, ring(zi, d, ZS), yi), device_id_type=MESH)

    for h in range(2):
        for d in (4, 3, 5, 2, 6, 1, 7):
            z_copy(h, d).start()

    for load in loads:
        load.wait()
    uft[...] = uf[...].T

    def x_copy(h, d):
        part = panel.at[xi, pl.ds(2 * h, 2)]
        return pltpu.make_async_remote_copy(
            src_ref=part, dst_ref=part, send_sem=xs_sem.at[h, d], recv_sem=xr_sem.at[h, d],
            device_id=at_users(ring(xi, d, XS), zi, yi), device_id_type=MESH)

    def pass_on(h):
        for d in range(1, ZS):
            z_copy(h, d).wait_recv()
        for d in (1, 3, 2):
            x_copy(h, d).start()

    pass_on(0)

    bits = jnp.left_shift(jnp.int32(1), lax.broadcasted_iota(jnp.int32, (1, 8, 128), 1))

    def g_copy(h, d):
        return pltpu.make_async_remote_copy(
            src_ref=grad_out.at[h, d], dst_ref=grad_in.at[h, d],
            send_sem=gs_sem.at[h, d], recv_sem=gr_sem.at[h, d],
            device_id=at_users(ring(xi, d, XS), zi, yi), device_id_type=MESH)

    def chunk(q, h):
        pair = panel[q, pl.ds(2 * h, 2)].reshape(2 * QROWS, RANK)
        lanes = pl.ds(pl.multiple_of(lax.rem(q, 2) * 128, 128), 128)
        p = lax.div(q, 2)
        for u in range(UTILES):
            span = pl.ds(u * TILE, TILE)
            predicted = lax.dot_general(
                uf[span, :], pair, (((1,), (1,)), ((), ())), preferred_element_type=F32)
            parts = []
            for k in range(2):
                first = (2 * h + k) * SLOTS
                slot = first + slots[first + 2 * u + p]
                live = lives[first + 2 * u + p]
                words = mask_v[slot, :, lanes] & live
                seen = (jnp.broadcast_to(words[:, None, :], (32, 8, 128)) & bits) != 0
                gap = predicted[:, k * 128:(k + 1) * 128] - rat_v[slot, :, lanes].astype(F32)
                kept = jnp.where(seen, gap.reshape(32, 8, 128), 0.0)
                parts.append(kept.reshape(TILE, 128).astype(BF16))
            errors = jnp.concatenate(parts, axis=1)
            err[span, :] = errors
            user_sum[span, :] += jnp.dot(errors, pair, preferred_element_type=F32)
        gacc[...] = jnp.dot(uft[...], err[...], preferred_element_type=F32)
        return gacc[...].T.reshape(2, QROWS, RANK)

    @pl.loop(0, 8)
    def _(c):
        h = lax.div(c, 4)
        k = lax.rem(c, 4)
        d = jnp.where(h == 0, jnp.where(k == 3, 2, jnp.where(k == 2, 3, k)),
                      jnp.where(k == 3, 0, jnp.where(k == 2, 3, 2 - k)))
        q = ring(xi, d, XS)

        @pl.when(c == 1)
        def _():
            pass_on(1)

        @pl.when(d != 0)
        def _():
            x_copy(h, XS - d).wait_recv()

        grad = chunk(q, h)

        @pl.when(d == 0)
        def _():
            own_grad[h] = grad

        @pl.when(d != 0)
        def _():
            grad_out[h, d] = grad.astype(BF16)
            g_copy(h, d).start()

    def u_copy(d):
        return pltpu.make_async_remote_copy(
            src_ref=user_out.at[d], dst_ref=user_in.at[d],
            send_sem=us_sem.at[d], recv_sem=ur_sem.at[d],
            device_id={"items": ring(it, d, ITEMS)}, device_id_type=MESH)

    def zy_copy(h, d):
        return pltpu.make_async_remote_copy(
            src_ref=zy_out.at[h, d], dst_ref=zy_in.at[h, d],
            send_sem=zys_sem.at[h, d], recv_sem=zyr_sem.at[h, d],
            device_id={"users": xi * ZY + ring(zy, d, ZY)}, device_id_type=MESH)

    share = 2 * TILE
    for h in range(2):
        for d in range(1, XS):
            g_copy(h, d).wait_recv()
        sums[h] = own_grad[h] + (
            grad_in[h, 1].astype(F32) + grad_in[h, 2].astype(F32) + grad_in[h, 3].astype(F32))
        for d in range(1, ZY):
            rows = pl.ds(pl.multiple_of(ring(zy, d, ZY) * ROWS, ROWS), ROWS)
            zy_out[h, d] = sums[h, :, rows, :].reshape(2 * ROWS, RANK).astype(BF16)
        for d in (8, 7, 9, 6, 10, 5, 11, 4, 12, 3, 13, 2, 14, 1, 15):
            zy_copy(h, d).start()
        if h == 0:
            for d in (2, 3, 1):
                rows = pl.ds(pl.multiple_of(ring(it, d, ITEMS) * share, share), share)
                user_out[d] = user_sum[rows, :].astype(BF16)
                u_copy(d).start()

    my_share = pl.ds(pl.multiple_of(it * share, share), share)
    for d in range(1, ITEMS):
        u_copy(d).wait_recv()
    user_grad[...] = (user_sum[my_share, :] + (
        user_in[1].astype(F32) + user_in[2].astype(F32) + user_in[3].astype(F32))) * (1.0 / 32.0)

    step_rate = 8.0 / math.sqrt(TILE * XS * ZY)
    mine_rows = pl.ds(pl.multiple_of(zy * ROWS, ROWS), ROWS)
    for h in range(2):
        total = sums[h, :, mine_rows, :].reshape(2 * ROWS, RANK)
        for d in range(1, ZY):
            zy_copy(h, d).wait_recv()
            total = total + zy_in[h, d].astype(F32)
        pair = pl.ds(2 * h, 2)
        new_items[0, pair] = 0.95 * items[0, pair] - step_rate * total.reshape(2, ROWS, RANK)

    y_copy.wait_send()
    for h in range(2):
        for d in range(1, ZS):
            z_copy(h, d).wait_send()
        for d in range(1, XS):
            x_copy(h, d).wait_send()
            g_copy(h, d).wait_send()
        for d in range(1, ZY):
            zy_copy(h, d).wait_send()
    for d in range(1, ITEMS):
        u_copy(d).wait_send()


def shards(user_factors, item_factors, tile_user, tile_item, tile_count, ratings, mask):
    vmem = pl.BlockSpec(memory_space=pltpu.VMEM)
    hbm = pl.BlockSpec(memory_space=pl.ANY)
    dma = pltpu.SemaphoreType.DMA
    return pl.pallas_call(
        kernel,
        out_shape=(
            jax.ShapeDtypeStruct(item_factors.shape, F32),
            jax.ShapeDtypeStruct((user_factors.shape[0] // ITEMS, RANK), F32),
        ),
        in_specs=[hbm] * 7,
        out_specs=(vmem, vmem),
        scratch_shapes=[
            pltpu.SMEM(tile_user.shape, jnp.int32),
            pltpu.SMEM(tile_item.shape, jnp.int32),
            pltpu.SMEM(tile_count.shape, jnp.int32),
            pltpu.VMEM(item_factors.shape, F32),
            pltpu.SMEM((STEPS * SLOTS,), jnp.int32),
            pltpu.SMEM((STEPS * SLOTS,), jnp.int32),
            pltpu.SMEM((STEPS * SLOTS,), jnp.int32),
            pltpu.VMEM((STEPS * SLOTS, TILE, TILE), BF16),
            pltpu.VMEM((STEPS * SLOTS, TILE // 8, TILE), jnp.int32),
            pltpu.VMEM((UTILES * TILE, RANK), BF16),
            pltpu.VMEM((RANK, UTILES * TILE), BF16),
            pltpu.VMEM((XS, STEPS, QROWS, RANK), BF16),
            pltpu.VMEM((STEPS, ROWS, RANK), F32),
            pltpu.VMEM((UTILES * TILE, 2 * QROWS), BF16),
            pltpu.VMEM((RANK, 2 * QROWS), F32),
            pltpu.VMEM((2, 2, QROWS, RANK), F32),
            pltpu.VMEM((2, XS, 2, QROWS, RANK), BF16),
            pltpu.VMEM((2, XS, 2, QROWS, RANK), BF16),
            pltpu.VMEM((2, 2, QROWS, RANK), F32),
            pltpu.VMEM((2, ZY, 2 * ROWS, RANK), BF16),
            pltpu.VMEM((2, ZY, 2 * ROWS, RANK), BF16),
            pltpu.VMEM((UTILES * TILE, RANK), F32),
            pltpu.VMEM((ITEMS, 2 * TILE, RANK), BF16),
            pltpu.VMEM((ITEMS, 2 * TILE, RANK), BF16),
            dma((13,)), dma((2,)), dma((2, ZS)), dma((2, ZS)),
            dma((2, XS)), dma((2, XS)), dma((2, XS)), dma((2, XS)),
            dma((2, ZY)), dma((2, ZY)), dma((ITEMS,)), dma((ITEMS,)),
        ],
        compiler_params=pltpu.CompilerParams(
            collective_id=0, has_side_effects=True, vmem_limit_bytes=67043328),
        name="factor_step",
    )(tile_user, tile_item, tile_count, item_factors, user_factors, ratings, mask)


def solution(mesh):
    return jax.shard_map(
        shards,
        mesh=mesh,
        in_specs=(
            P("users", None),
            P("items", None, "users", None),
            P("users", "items", None, None),
            P("users", "items", None, None),
            P("users", "items", None),
            P("users", "items", None, None, None, None),
            P("users", "items", None, None, None, None),
        ),
        out_specs=(P("items", None, "users", None), P(("users", "items"), None)),
        check_vma=False,
    )
```

```python
import functools
import math

import jax
import jax.numpy as jnp
from jax import lax
from jax.experimental import pallas as pl
from jax.experimental.pallas import tpu as pltpu
from jax.sharding import PartitionSpec as P

MESH = pl.DeviceIdType.MESH
XS, ZS, YS = 4, 8, 2
ITEMS = 4
STEPS = 4
SLOTS = 16
TILE = 256
UTILES = 8
RANK = 128
ROWS = 8
QROWS = 128
ZY = ZS * YS
F32, BF16 = jnp.float32, jnp.bfloat16


def kernel(
    tile_user_hbm, tile_item_hbm, tile_count_hbm, items_hbm, factors, ratings, mask,
    new_items, user_grad,
    tile_user, tile_item, tile_count, items,
    slots, lives, cells, rat_v, mask_v, uf, uft, panel, other, err, gacc,
    own_grad, grad_out, grad_in, sums, zy_out, zy_in, user_part, user_out, user_in,
    load_sem, y_sem, zs_sem, zr_sem, xs_sem, xr_sem, gs_sem, gr_sem,
    zys_sem, zyr_sem, us_sem, ur_sem,
):
    me = lax.axis_index("users")
    it = lax.axis_index("items")
    xi = lax.div(me, ZY)
    zy = lax.rem(me, ZY)
    zi = lax.div(zy, YS)
    yi = lax.rem(zy, YS)

    twin = it + 1 - 2 * lax.rem(it, 2)
    across = lax.rem(it + 2, ITEMS)
    far = lax.rem(twin + 2, ITEMS)

    def at_users(x, z, y):
        return {"users": x * ZY + z * YS + y}

    def ring(value, step, size):
        return lax.rem(value + step, size)

    tables = [
        pltpu.make_async_copy(tile_user_hbm, tile_user, load_sem.at[9]),
        pltpu.make_async_copy(tile_item_hbm, tile_item, load_sem.at[10]),
        pltpu.make_async_copy(tile_count_hbm, tile_count, load_sem.at[11]),
        pltpu.make_async_copy(items_hbm, items, load_sem.at[12]),
    ]
    loads = [pltpu.make_async_copy(factors, uf, load_sem.at[8])]
    for s in range(STEPS):
        rows = pl.ds(s * SLOTS, SLOTS)
        loads.append(pltpu.make_async_copy(mask.at[0, 0, s], mask_v.at[rows], load_sem.at[s]))
        loads.append(pltpu.make_async_copy(ratings.at[0, 0, s], rat_v.at[rows], load_sem.at[4 + s]))

    barrier = pltpu.get_barrier_semaphore()
    greeted = 0
    pl.semaphore_signal(barrier, inc=1, device_id=at_users(xi, zi, 1 - yi), device_id_type=MESH)
    greeted += 1
    for d in range(1, ZS):
        pl.semaphore_signal(barrier, inc=1, device_id=at_users(xi, ring(zi, d, ZS), yi), device_id_type=MESH)
        greeted += 1
    for d in range(1, XS):
        pl.semaphore_signal(barrier, inc=1, device_id={"users": ring(xi, d, XS) * ZY + zy}, device_id_type=MESH)
        greeted += 1
    for partner in (twin, across):
        pl.semaphore_signal(barrier, inc=1, device_id={"items": partner}, device_id_type=MESH)
        greeted += 1
    for load in tables + loads:
        load.start()
    for load in tables:
        load.wait()

    for s in range(STEPS):
        for t in range(SLOTS):
            cell = tile_user[0, 0, s, t] * 2 + tile_item[0, 0, s, t]
            cells[s * SLOTS + t] = jnp.where(t < tile_count[0, 0, s], cell, -1)

    @pl.loop(0, STEPS * SLOTS)
    def _(idx):
        first = lax.div(idx, SLOTS) * SLOTS
        cell = lax.rem(idx, SLOTS)
        slot = jnp.int32(0)
        live = jnp.int32(0)
        for t in range(SLOTS):
            hit = cells[first + t] == cell
            slot = jnp.where(hit, t, slot)
            live = jnp.where(hit, -1, live)
        slots[idx] = slot
        lives[idx] = live

    pl.semaphore_wait(barrier, greeted)

    y_copy = pltpu.make_async_remote_copy(
        src_ref=items_hbm.at[0], dst_ref=other, send_sem=y_sem.at[0], recv_sem=y_sem.at[1],
        device_id=at_users(xi, zi, 1 - yi), device_id_type=MESH)
    y_copy.start()

    y_copy.wait_recv()
    mine = items[0]
    theirs = other[...]
    low = jnp.where(yi == 0, mine, theirs)
    high = jnp.where(yi == 0, theirs, mine)
    my_rows = pl.ds(pl.multiple_of(zi * 16, 16), 16)
    panel[xi, :, my_rows, :] = jnp.concatenate([low, high], axis=1).astype(BF16)

    def z_copy(h, d):
        part = panel.at[xi, pl.ds(2 * h, 2), my_rows, :]
        return pltpu.make_async_remote_copy(
            src_ref=part, dst_ref=part, send_sem=zs_sem.at[h, d], recv_sem=zr_sem.at[h, d],
            device_id=at_users(xi, ring(zi, d, ZS), yi), device_id_type=MESH)

    for h in range(2):
        for d in (4, 3, 5, 2, 6, 1, 7):
            z_copy(h, d).start()

    for load in loads:
        load.wait()
    uft[...] = uf[...].T

    def x_copy(h, d):
        part = panel.at[xi, pl.ds(2 * h, 2)]
        return pltpu.make_async_remote_copy(
            src_ref=part, dst_ref=part, send_sem=xs_sem.at[h, d], recv_sem=xr_sem.at[h, d],
            device_id=at_users(ring(xi, d, XS), zi, yi), device_id_type=MESH)

    def pass_on(h):
        for d in range(1, ZS):
            z_copy(h, d).wait_recv()
        for d in (1, 3, 2):
            x_copy(h, d).start()

    pass_on(0)

    bits = jnp.left_shift(jnp.int32(1), lax.broadcasted_iota(jnp.int32, (1, 8, 128), 1))

    def g_copy(h, d):
        return pltpu.make_async_remote_copy(
            src_ref=grad_out.at[h, d], dst_ref=grad_in.at[h, d],
            send_sem=gs_sem.at[h, d], recv_sem=gr_sem.at[h, d],
            device_id=at_users(ring(xi, d, XS), zi, yi), device_id_type=MESH)

    def chunk(q, h):
        pair = panel[q, pl.ds(2 * h, 2)].reshape(2 * QROWS, RANK)
        columns = pl.ds(pl.multiple_of((2 * q + h) * 2 * QROWS, 2 * QROWS), 2 * QROWS)
        lanes = pl.ds(pl.multiple_of(lax.rem(q, 2) * 128, 128), 128)
        p = lax.div(q, 2)
        for u in range(UTILES):
            span = pl.ds(u * TILE, TILE)
            predicted = lax.dot_general(
                uf[span, :], pair, (((1,), (1,)), ((), ())), preferred_element_type=F32)
            parts = []
            for k in range(2):
                first = (2 * h + k) * SLOTS
                slot = first + slots[first + 2 * u + p]
                live = lives[first + 2 * u + p]
                words = mask_v[slot, :, lanes] & live
                seen = (jnp.broadcast_to(words[:, None, :], (32, 8, 128)) & bits) != 0
                gap = predicted[:, k * 128:(k + 1) * 128] - rat_v[slot, :, lanes].astype(F32)
                kept = jnp.where(seen, gap.reshape(32, 8, 128), 0.0)
                parts.append(kept.reshape(TILE, 128).astype(BF16))
            err[span, columns] = jnp.concatenate(parts, axis=1)
        gacc[...] = jnp.dot(uft[...], err[:, columns], preferred_element_type=F32)
        return gacc[...].T.reshape(2, QROWS, RANK)

    @pl.loop(0, 8)
    def _(c):
        h = jnp.where(c < 2, c, jnp.where(c < 5, 0, 1))
        d = jnp.where(c < 2, 0, jnp.where(c < 5, jnp.where(c == 2, 1, 6 - c), c - 4))
        q = ring(xi, d, XS)

        @pl.when(c == 1)
        def _():
            pass_on(1)

        @pl.when(d != 0)
        def _():
            x_copy(h, XS - d).wait_recv()

        grad = chunk(q, h)

        @pl.when(d == 0)
        def _():
            own_grad[h] = grad

        @pl.when(d != 0)
        def _():
            grad_out[h, d] = grad.astype(BF16)
            g_copy(h, d).start()

    def zy_copy(h, d):
        return pltpu.make_async_remote_copy(
            src_ref=zy_out.at[h, d], dst_ref=zy_in.at[h, d],
            send_sem=zys_sem.at[h, d], recv_sem=zyr_sem.at[h, d],
            device_id={"users": xi * ZY + ring(zy, d, ZY)}, device_id_type=MESH)

    def exchange(h):
        for d in range(1, XS):
            g_copy(h, d).wait_recv()
        sums[h] = own_grad[h] + (
            grad_in[h, 1].astype(F32) + grad_in[h, 2].astype(F32) + grad_in[h, 3].astype(F32))
        for d in range(1, ZY):
            rows = pl.ds(pl.multiple_of(ring(zy, d, ZY) * ROWS, ROWS), ROWS)
            zy_out[h, d] = sums[h, :, rows, :].reshape(2 * ROWS, RANK).astype(BF16)
        for d in (8, 7, 9, 6, 10, 5, 11, 4, 12, 3, 13, 2, 14, 1, 15):
            zy_copy(h, d).start()

    share = 2 * TILE

    def user_terms(owner):
        rows = pl.ds(pl.multiple_of(owner * share, share), share)
        every = panel[...].reshape(STEPS * XS * QROWS, RANK)
        return jnp.dot(err[rows, :], every, preferred_element_type=F32)

    def u_copy(k):
        return pltpu.make_async_remote_copy(
            src_ref=user_out.at[k], dst_ref=user_in.at[k],
            send_sem=us_sem.at[k], recv_sem=ur_sem.at[k],
            device_id={"items": across if k == 2 else twin}, device_id_type=MESH)

    user_out[0] = user_terms(far).astype(BF16)
    u_copy(0).start()
    user_out[1] = user_terms(twin).astype(BF16)
    u_copy(1).start()
    exchange(0)
    user_part[0] = user_terms(across)
    user_part[1] = user_terms(it)
    exchange(1)
    u_copy(0).wait_recv()
    user_out[2] = (user_part[0] + user_in[0].astype(F32)).astype(BF16)
    u_copy(2).start()

    u_copy(1).wait_recv()
    user_part[1] = user_part[1] + user_in[1].astype(F32)
    u_copy(2).wait_recv()
    user_grad[...] = (user_part[1] + user_in[2].astype(F32)) * (1.0 / 32.0)

    step_rate = 8.0 / math.sqrt(TILE * XS * ZY)
    mine_rows = pl.ds(pl.multiple_of(zy * ROWS, ROWS), ROWS)
    for h in range(2):
        total = sums[h, :, mine_rows, :].reshape(2 * ROWS, RANK)
        for d in range(1, ZY):
            zy_copy(h, d).wait_recv()
            total = total + zy_in[h, d].astype(F32)
        pair = pl.ds(2 * h, 2)
        new_items[0, pair] = 0.95 * items[0, pair] - step_rate * total.reshape(2, ROWS, RANK)

    y_copy.wait_send()
    for h in range(2):
        for d in range(1, ZS):
            z_copy(h, d).wait_send()
        for d in range(1, XS):
            x_copy(h, d).wait_send()
            g_copy(h, d).wait_send()
        for d in range(1, ZY):
            zy_copy(h, d).wait_send()
    for k in range(3):
        u_copy(k).wait_send()


def shards(user_factors, item_factors, tile_user, tile_item, tile_count, ratings, mask):
    vmem = pl.BlockSpec(memory_space=pltpu.VMEM)
    hbm = pl.BlockSpec(memory_space=pl.ANY)
    dma = pltpu.SemaphoreType.DMA
    operands = (tile_user, tile_item, tile_count, item_factors, user_factors, ratings, mask)
    return pl.pallas_call(
        kernel,
        out_shape=(
            jax.ShapeDtypeStruct(item_factors.shape, F32),
            jax.ShapeDtypeStruct((user_factors.shape[0] // ITEMS, RANK), F32),
        ),
        in_specs=[hbm] * 7,
        out_specs=(vmem, vmem),
        scratch_shapes=[
            pltpu.SMEM(tile_user.shape, jnp.int32),
            pltpu.SMEM(tile_item.shape, jnp.int32),
            pltpu.SMEM(tile_count.shape, jnp.int32),
            pltpu.VMEM(item_factors.shape, F32),
            pltpu.SMEM((STEPS * SLOTS,), jnp.int32),
            pltpu.SMEM((STEPS * SLOTS,), jnp.int32),
            pltpu.SMEM((STEPS * SLOTS,), jnp.int32),
            pltpu.VMEM((STEPS * SLOTS, TILE, TILE), BF16),
            pltpu.VMEM((STEPS * SLOTS, TILE // 8, TILE), jnp.int32),
            pltpu.VMEM((UTILES * TILE, RANK), BF16),
            pltpu.VMEM((RANK, UTILES * TILE), BF16),
            pltpu.VMEM((XS, STEPS, QROWS, RANK), BF16),
            pltpu.VMEM((STEPS, ROWS, RANK), F32),
            pltpu.VMEM((UTILES * TILE, STEPS * XS * QROWS), BF16),
            pltpu.VMEM((RANK, 2 * QROWS), F32),
            pltpu.VMEM((2, 2, QROWS, RANK), F32),
            pltpu.VMEM((2, XS, 2, QROWS, RANK), BF16),
            pltpu.VMEM((2, XS, 2, QROWS, RANK), BF16),
            pltpu.VMEM((2, 2, QROWS, RANK), F32),
            pltpu.VMEM((2, ZY, 2 * ROWS, RANK), BF16),
            pltpu.VMEM((2, ZY, 2 * ROWS, RANK), BF16),
            pltpu.VMEM((2, 2 * TILE, RANK), F32),
            pltpu.VMEM((3, 2 * TILE, RANK), BF16),
            pltpu.VMEM((3, 2 * TILE, RANK), BF16),
            dma((13,)), dma((2,)), dma((2, ZS)), dma((2, ZS)),
            dma((2, XS)), dma((2, XS)), dma((2, XS)), dma((2, XS)),
            dma((2, ZY)), dma((2, ZY)), dma((3,)), dma((3,)),
        ],
        compiler_params=pltpu.CompilerParams(
            collective_id=0, has_side_effects=True, vmem_limit_bytes=48 * 2**20),
        name="factor_step",
    )(*(pltpu.with_memory_space_constraint(operand, pltpu.HBM) for operand in operands))


def solution(mesh):
    return jax.shard_map(
        shards,
        mesh=mesh,
        in_specs=(
            P("users", None),
            P("items", None, "users", None),
            P("users", "items", None, None),
            P("users", "items", None, None),
            P("users", "items", None),
            P("users", "items", None, None, None, None),
            P("users", "items", None, None, None, None),
        ),
        out_specs=(P("items", None, "users", None), P(("users", "items"), None)),
        check_vma=False,
    )
```
